256 devices in a mesh: view: 8 (over y, x_lo), band: 32 (over x_hi, z, core).
Axes of the slice: x: 4 (x_hi: 2, x_lo: 2; x = x_hi * 2 + x_lo), y: 4, z: 8, core: 2. Of those that a mesh axis runs over, the one named last changes fastest.
Arguments:
- features: float32 [8, 256, 512, 128], P('view', 'band'), may hold values from -6 to 6
- tempers: float32 [8, 256, 512], P('view', 'band'), may hold values from 0.5 to 80
- partners: int32 [8, 2], replicated, may hold values from 0 to 7, as said below
- conv_one: bfloat16 [3, 3, 128, 128], replicated, may hold values from -0.1875 to 0.1875
- conv_two: bfloat16 [3, 3, 128, 128], replicated, may hold values from -0.1875 to 0.1875
- query_weight: bfloat16 [128, 128], replicated, may hold values from -0.5 to 0.5
- key_weight: bfloat16 [128, 128], replicated, may hold values from -0.5 to 0.5
- value_weight: bfloat16 [128, 128], replicated, may hold values from -0.5 to 0.5
- out_weight: bfloat16 [128, 128], replicated, may hold values from -0.5 to 0.5
- norm_gain: float32 [128], replicated, may hold values from 0.25 to 1.75
- message_gain: float32 [128], replicated, may hold values from 0.25 to 1.75
Outputs:
- refined: float32 [8, 256, 512, 128], P('view', 'band')
The draws below stay inside these ranges and needn't reach their ends.
Inputs may be any that keep to these rules, and one draw needn't show every extreme that they name: Column 0 and column 1 are each a permutation of the 8 views; a view is never its own partner, and its two partners differ. At least one view has as its first partner the view 4 positions away from it (modulo 8).
All inputs are finite; a program needn't handle non-finite values.
Results may differ from the reference program's by a relative error of at most 0.0065.
Values may be sent and summed in bfloat16 or wider, within the bound.
A program may use at most 64 MiB of HBM per device.

```python
import math
import jax
import jax.numpy as jnp
from jax import lax

FEATURES = 128
COLUMNS = 512
VIEWS = 8
HEIGHT = 256


def draw_tempers(key, part):
    level_key = jax.random.fold_in(jax.random.fold_in(key, 11), 0)
    shape = (VIEWS, HEIGHT, COLUMNS)
    levels = jnp.exp(jax.random.uniform(level_key, shape, jnp.float32, jnp.log(0.5), jnp.log(4.0)))
    return levels


def draw_partners(key, part):
    order_key, offset_key = jax.random.split(jax.random.fold_in(key, 23))
    ordering = jax.random.permutation(order_key, VIEWS).astype(jnp.int32)
    target = ((ordering[0] + VIEWS // 2) % VIEWS).astype(jnp.int32)
    found = jnp.argmax((ordering == target).astype(jnp.int32)).astype(jnp.int32)
    second_entry = ordering[1]
    ordering = ordering.at[1].set(target).at[found].set(second_entry)
    ordering = ordering.at[1].set(target)
    offset = jax.random.randint(offset_key, (), 2, VIEWS).astype(jnp.int32)
    positions = jnp.arange(VIEWS, dtype=jnp.int32)
    first_partner = jnp.zeros((VIEWS,), jnp.int32).at[ordering].set(ordering[(positions + 1) % VIEWS])
    second_partner = jnp.zeros((VIEWS,), jnp.int32).at[ordering].set(ordering[(positions + offset) % VIEWS])
    return jnp.stack([first_partner, second_partner], axis=1).astype(jnp.int32)


def block_levels(key, dims, pieces, low, high):
    level = 1.0
    for position, shards_of in pieces:
        draws = jax.random.uniform(jax.random.fold_in(jax.random.fold_in(key, 6), position), (shards_of,), jnp.float32, low / len(pieces), high / len(pieces))
        level = level * jnp.repeat(jnp.exp(draws), dims[position] // shards_of).reshape((-1,) + (1,) * (len(dims) - 1 - position))
    return level


def gaussian(stream_key, extent, scale, reach, shards=(), kind=jnp.bfloat16):
    drawn = jax.random.normal(stream_key, extent, jnp.float32) * scale
    if len(shards) > 0:
        drawn = block_levels(stream_key, extent, shards, -0.22, 0.18) * drawn
    return jnp.clip(drawn, min=-reach, max=reach).astype(kind)


def setup_inputs(seed: int = 0) -> dict:
    streams_of = jax.random.split(jax.random.key(seed), 12)
    features = gaussian(streams_of[0], (VIEWS, HEIGHT, COLUMNS, FEATURES), 1.0, 6.0, ((0, 8), (1, 32)), jnp.float32)
    tempers = draw_tempers(jax.random.fold_in(streams_of[11], 71), 0)
    partners = draw_partners(jax.random.fold_in(streams_of[11], 71), 0)
    conv_one = gaussian(streams_of[3], (3, 3, FEATURES, FEATURES), (9 * FEATURES) ** -0.5, 0.1875)
    conv_two = gaussian(streams_of[4], (3, 3, FEATURES, FEATURES), (9 * FEATURES) ** -0.5, 0.1875)
    query_weight = gaussian(streams_of[5], (FEATURES, FEATURES), FEATURES ** -0.5, 0.5)
    key_weight = gaussian(streams_of[6], (FEATURES, FEATURES), FEATURES ** -0.5, 0.5)
    value_weight = gaussian(streams_of[7], (FEATURES, FEATURES), FEATURES ** -0.5, 0.5)
    out_weight = gaussian(streams_of[8], (FEATURES, FEATURES), FEATURES ** -0.5, 0.5)
    norm_gain = jnp.clip(1.0 + 0.15 * jax.random.normal(streams_of[9], (FEATURES,), jnp.float32), 0.25, 1.75)
    message_gain = jnp.clip(1.0 + 0.15 * jax.random.normal(streams_of[10], (FEATURES,), jnp.float32), 0.25, 1.75)
    return dict(features=features, tempers=tempers, partners=partners, conv_one=conv_one, conv_two=conv_two, query_weight=query_weight, key_weight=key_weight, value_weight=value_weight, out_weight=out_weight, norm_gain=norm_gain, message_gain=message_gain)


epsilon = 1e-06

def root_norm(values, gain):
    mean_square = lax.optimization_barrier(jnp.mean(values * values, axis=-1, keepdims=True))
    return values * lax.rsqrt(mean_square + epsilon) * gain

def convolve(padded, kernel):
    leading = padded.shape[:-3]
    out_rows = padded.shape[-3] - 2
    columns = padded.shape[-2]
    channels = padded.shape[-1]
    widened = jnp.pad(padded, [(0, 0)] * len(leading) + [(0, 0), (1, 1), (0, 0)])
    summed = jnp.zeros(leading + (out_rows, columns, kernel.shape[-1]), jnp.float32)
    for row_tap in range(3):
        for col_tap in range(3):
            window = widened[..., row_tap:row_tap + out_rows, col_tap:col_tap + columns, :]
            product = jnp.dot(window.reshape(-1, channels), kernel[row_tap, col_tap], preferred_element_type=jnp.float32)
            summed = summed + product.reshape(summed.shape)
    return summed

def reference(features, tempers, partners, conv_one, conv_two, query_weight, key_weight, value_weight, out_weight, norm_gain, message_gain):
    row_pad = ((0, 0), (1, 1), (0, 0), (0, 0))
    first_input = jax.nn.silu(features).astype(jnp.bfloat16)
    state_one = features + convolve(jnp.pad(first_input, row_pad), conv_one)
    second_input = jax.nn.silu(state_one).astype(jnp.bfloat16)
    state_two = state_one + convolve(jnp.pad(second_input, row_pad), conv_two)
    normed = root_norm(state_two, norm_gain).astype(jnp.bfloat16)
    view_total, height, columns, channels = normed.shape
    flat_normed = normed.reshape(-1, channels)
    queries = jnp.dot(flat_normed, query_weight, preferred_element_type=jnp.float32).astype(jnp.bfloat16).reshape(normed.shape)
    key_all = jnp.dot(flat_normed, key_weight, preferred_element_type=jnp.float32).astype(jnp.bfloat16).reshape(normed.shape)
    value_all = jnp.dot(flat_normed, value_weight, preferred_element_type=jnp.float32).astype(jnp.bfloat16).reshape(normed.shape)
    key_pad = jnp.pad(key_all, row_pad)
    value_pad = jnp.pad(value_all, row_pad)
    factor = 1.0 / math.sqrt(channels)
    zero_index = jnp.zeros((), jnp.int32)

    def attend(flat_index):
        view_index = (flat_index // height).astype(jnp.int32)
        row_index = (flat_index % height).astype(jnp.int32)
        query_row = queries[view_index, row_index]
        temper_row = tempers[view_index, row_index] * factor
        summed = jnp.zeros((columns, channels), jnp.float32)
        for partner in range(2):
            source = partners[view_index, partner].astype(jnp.int32)
            starts = (source, row_index, zero_index, zero_index)
            key_rows = lax.dynamic_slice(key_pad, starts, (1, 3, columns, channels)).reshape(3 * columns, channels)
            value_rows = lax.dynamic_slice(value_pad, starts, (1, 3, columns, channels)).reshape(3 * columns, channels)
            scores = jnp.dot(query_row, key_rows.T, preferred_element_type=jnp.float32) * temper_row[:, None]
            row_peak = lax.optimization_barrier(jnp.max(scores, axis=-1, keepdims=True))
            lifted = jnp.exp(scores - row_peak)
            shares = (lifted / lax.optimization_barrier(jnp.sum(lifted, axis=-1, keepdims=True))).astype(jnp.bfloat16)
            blended = jnp.dot(shares, value_rows, preferred_element_type=jnp.float32).astype(jnp.bfloat16)
            summed = summed + jnp.dot(blended, out_weight, preferred_element_type=jnp.float32)
        return summed
    messages = lax.map(attend, jnp.arange(view_total * height, dtype=jnp.int32)).reshape(state_two.shape)
    return state_two + root_norm(messages, message_gain)
```

```python
import functools
import math

import jax
import jax.numpy as jnp
from jax import lax
from jax.experimental import pallas as pl
from jax.experimental.pallas import tpu as pltpu
from jax.sharding import PartitionSpec as P

MESH = pl.DeviceIdType.MESH
epsilon = 1e-06
ROW_STARTS = (2, 4, 6, 0)


def kernel(
    views,
    bands,
    feat_ref,
    temper_ref,
    partners_ref,
    conv_one_ref,
    conv_two_ref,
    query_w_ref,
    key_w_ref,
    value_w_ref,
    out_w_ref,
    norm_gain_ref,
    message_gain_ref,
    out_ref,
    state,
    taps_one,
    taps_two,
    kernel_one,
    kernel_two,
    kv_w,
    out_w2,
    halo_send_one,
    halo_recv_one,
    halo_send_two,
    halo_recv_two,
    normed,
    gather_a,
    gather_b,
    gather_c,
    gather_d,
    deal,
    pair,
    query,
    keys,
    values,
    temper_wide,
    scores,
    shares,
    load_sem,
    halo_ssem,
    halo_rsem,
    one_ssem,
    one_rsem,
    two_ssem,
    two_rsem,
    edge_ssem,
    edge_rsem,
):
    rows, columns, channels = state.shape
    chunk = columns // views
    view = lax.axis_index("view")
    band = lax.axis_index("band")
    up = lax.rem(band + bands - 1, bands)
    down = lax.rem(band + 1, bands)
    gathers = (gather_a, gather_b, gather_c, gather_d)

    def other(k):
        return lax.rem(view + k, views)

    spans = ((0, 1), (rows - 1, 1), (1, rows - 2))
    loads = [
        pltpu.make_async_copy(
            feat_ref.at[0, pl.ds(s, n)], state.at[pl.ds(s, n)], load_sem.at[i]
        )
        for i, (s, n) in enumerate(spans)
    ]
    for load in loads:
        load.start()
    barrier = pltpu.get_barrier_semaphore()
    for k in range(1, views):
        pl.semaphore_signal(barrier, inc=1, device_id={"view": other(k)}, device_id_type=MESH)
    for near in (up, down):
        pl.semaphore_signal(barrier, inc=1, device_id={"band": near}, device_id_type=MESH)

    def silu(x):
        return x / (1.0 + jnp.exp(-x))

    place = lax.broadcasted_iota(jnp.int32, (columns, channels), 0)

    def store_taps(taps, row, x):
        before = jnp.where(place == 0, 0.0, pltpu.roll(x, 1, 0))
        after = jnp.where(place == columns - 1, 0.0, pltpu.roll(x, columns - 1, 0))
        taps[row, :, 0:channels] = before.astype(jnp.bfloat16)
        taps[row, :, channels : 2 * channels] = x.astype(jnp.bfloat16)
        taps[row, :, 2 * channels : 3 * channels] = after.astype(jnp.bfloat16)

    def halo_copy(stage, side, send, recv):
        return pltpu.make_async_remote_copy(
            src_ref=send.at[side],
            dst_ref=recv.at[side],
            send_sem=halo_ssem.at[stage, side],
            recv_sem=halo_rsem.at[stage, side],
            device_id={"band": down if side == 0 else up},
            device_id_type=MESH,
        )

    def edge_taps(taps, recv):
        above = recv[0].astype(jnp.float32)
        store_taps(taps, 0, jnp.where(band == 0, 0.0, above))
        below = recv[1].astype(jnp.float32)
        store_taps(taps, rows + 1, jnp.where(band == bands - 1, 0.0, below))

    def conv_pair(taps, weights, first):
        wide = jnp.concatenate([taps[first + i] for i in range(4)], axis=1)
        return jnp.dot(wide, weights[...], preferred_element_type=jnp.float32)

    loads[0].wait()
    loads[1].wait()
    for row, side in ((0, 1), (rows - 1, 0)):
        x = silu(state[row])
        halo_send_one[side] = x.astype(jnp.bfloat16)
        store_taps(taps_one, row + 1, x)
    pl.semaphore_wait(barrier, views + 1)
    for side in range(2):
        halo_copy(0, side, halo_send_one, halo_recv_one).start()

    for source, target in ((conv_one_ref, kernel_one), (conv_two_ref, kernel_two)):
        for i in range(4):
            for b in range(3):
                at = (i * 3 + b) * channels
                for o in range(2):
                    if 0 <= i - o <= 2:
                        block = source[i - o, b]
                    else:
                        block = jnp.zeros((channels, channels), jnp.bfloat16)
                    target[at : at + channels, o * channels : (o + 1) * channels] = block
    kv_w[:, 0:channels] = key_w_ref[...]
    kv_w[:, channels : 2 * channels] = value_w_ref[...]
    out_w2[0:channels, :] = out_w_ref[...]
    out_w2[channels : 2 * channels, :] = out_w_ref[...]

    loads[2].wait()

    def silu_row(row, _):
        store_taps(taps_one, row + 1, silu(state[row]))
        return 0

    lax.fori_loop(1, rows - 1, silu_row, 0)

    def conv_one_step(step, _):
        first = lax.rem(2 + 2 * step, rows)

        @pl.when(step == 2)
        def _():
            for side in range(2):
                halo_copy(0, side, halo_send_one, halo_recv_one).wait_recv()
            edge_taps(taps_one, halo_recv_one)

        added = conv_pair(taps_one, kernel_one, first)
        for o in range(2):
            x = state[first + o] + added[:, o * channels : (o + 1) * channels]
            state[first + o] = x
            store_taps(taps_two, first + o + 1, silu(x))

        return 0

    lax.fori_loop(0, 4, conv_one_step, 0)
    halo_send_two[0] = taps_two[rows, :, channels : 2 * channels]
    halo_send_two[1] = taps_two[1, :, channels : 2 * channels]
    for side in range(2):
        halo_copy(1, side, halo_send_two, halo_recv_two).start()

    def one_copy(g, k):
        first = ROW_STARTS[g]
        return pltpu.make_async_remote_copy(
            src_ref=normed.at[pl.ds(first, 2), pl.ds(pl.multiple_of(other(k) * chunk, chunk), chunk)],
            dst_ref=gathers[g].at[view],
            send_sem=one_ssem.at[g, k],
            recv_sem=one_rsem.at[g, view],
            device_id={"view": other(k)},
            device_id_type=MESH,
        )

    def one_arrival(g, k):
        return pltpu.make_async_remote_copy(
            src_ref=gathers[g].at[other(k)],
            dst_ref=gathers[g].at[other(k)],
            send_sem=one_ssem.at[g, k],
            recv_sem=one_rsem.at[g, other(k)],
            device_id={"view": other(k)},
            device_id_type=MESH,
        )

    def conv_two_step(step, _):
        first = lax.rem(2 + 2 * step, rows)

        @pl.when(step == 2)
        def _():
            for side in range(2):
                halo_copy(1, side, halo_send_two, halo_recv_two).wait_recv()
            edge_taps(taps_two, halo_recv_two)

        added = conv_pair(taps_two, kernel_two, first)
        for o in range(2):
            x = state[first + o] + added[:, o * channels : (o + 1) * channels]
            state[first + o] = x
            scale = lax.rsqrt(jnp.mean(x * x, axis=-1, keepdims=True) + epsilon)
            normed[first + o] = (x * scale * norm_gain_ref[...]).astype(jnp.bfloat16)

        for g in range(4):

            @pl.when(step == g)
            def _():
                for k in range(1, views):
                    one_copy(g, k).start()

        return 0

    lax.fori_loop(0, 4, conv_two_step, 0)

    own = pl.ds(pl.multiple_of(view * chunk, chunk), chunk)

    def two_copy(g, k):
        first = ROW_STARTS[g]
        return pltpu.make_async_remote_copy(
            src_ref=deal.at[g, k],
            dst_ref=pair.at[:, pl.ds(first + 1, 2), own],
            send_sem=two_ssem.at[g, k],
            recv_sem=two_rsem.at[g, view],
            device_id={"view": other(k)},
            device_id_type=MESH,
        )

    def two_arrival(g, k):
        first = ROW_STARTS[g]
        theirs = pl.ds(pl.multiple_of(other(k) * chunk, chunk), chunk)
        return pltpu.make_async_remote_copy(
            src_ref=deal.at[g, k],
            dst_ref=pair.at[:, pl.ds(first + 1, 2), theirs],
            send_sem=two_ssem.at[g, k],
            recv_sem=two_rsem.at[g, other(k)],
            device_id={"view": other(k)},
            device_id_type=MESH,
        )

    for g in range(4):
        first = ROW_STARTS[g]
        gathers[g][view] = normed[pl.ds(first, 2), own]
        for k in range(1, views):
            one_arrival(g, k).wait_recv()
        for k in range(1, views):
            for p in range(2):
                deal[g, k, p] = gathers[g][partners_ref[other(k), p]]
        for k in range(1, views):
            two_copy(g, k).start()
        for p in range(2):
            pair[p, pl.ds(first + 1, 2), own] = gathers[g][partners_ref[view, p]]

    def query_row(row, _):
        query[row] = jnp.dot(
            normed[row], query_w_ref[...], preferred_element_type=jnp.float32
        ).astype(jnp.bfloat16)
        return 0

    lax.fori_loop(0, rows, query_row, 0)

    factor = 1.0 / math.sqrt(channels) * math.log2(math.e)
    for c in range(columns // 128):
        at = slice(c * 128, (c + 1) * 128)
        turned = jnp.concatenate([temper_ref[0, :, at] * factor] * (128 // rows), axis=0).T
        for row in range(rows):
            temper_wide[row, at, :] = jnp.broadcast_to(turned[:, row : row + 1], (128, channels))

    def fill_ones(row, _):
        for p in range(2):
            values[p, row, :, channels : 2 * channels] = jnp.ones(
                (columns, channels), jnp.bfloat16
            )
        return 0

    lax.fori_loop(0, rows + 2, fill_ones, 0)

    def project(row, keep=None):
        for p in range(2):
            both = jnp.dot(pair[p, row], kv_w[...], preferred_element_type=jnp.float32)
            if keep is not None:
                both = jnp.where(keep, both, 0.0)
            both = both.astype(jnp.bfloat16)
            keys[p, row] = both[:, 0:channels]
            values[p, row, :, 0:channels] = both[:, channels : 2 * channels]

    def edge_copy(side):
        source, target = ((rows, 0), (1, rows + 1))[side]
        return pltpu.make_async_remote_copy(
            src_ref=pair.at[:, source],
            dst_ref=pair.at[:, target],
            send_sem=edge_ssem.at[side],
            recv_sem=edge_rsem.at[side],
            device_id={"band": down if side == 0 else up},
            device_id_type=MESH,
        )

    def arrive(g):
        for k in range(1, views):
            two_arrival(g, k).wait_recv()
        if ROW_STARTS[g] == 0:
            edge_copy(1).start()
        if ROW_STARTS[g] == rows - 2:
            edge_copy(0).start()

        def one_row(i, _):
            project(ROW_STARTS[g] + 1 + i)
            return 0

        lax.fori_loop(0, 2, one_row, 0)

    def attend(step, _):
        late = step // 4
        row = (1 - late) * (3 + step) + late * lax.rem(14 - step, 8)

        @pl.when(step == 0)
        def _():
            arrive(0)
            arrive(1)

        @pl.when(step == 2)
        def _():
            arrive(2)

        @pl.when(step == 4)
        def _():
            arrive(3)

        @pl.when(step == 6)
        def _():
            for side in range(2):
                edge_copy(side).wait_recv()
            project(0, band > 0)
            project(rows + 1, band < bands - 1)

        temper = temper_wide[row]
        blended = []
        for p in range(2):
            peak = None
            for a in range(3):
                for j in range(columns // 256):
                    at = a * columns + j * 256
                    part = lax.dot_general(
                        query[row],
                        keys[p, row + a, j * 256 : (j + 1) * 256, :],
                        (((1,), (1,)), ((), ())),
                        preferred_element_type=jnp.float32,
                    )
                    scores[p, :, at : at + 256] = part
                    part = jnp.maximum(part[:, 0:128], part[:, 128:256])
                    peak = part if peak is None else jnp.maximum(peak, part)
            top = jnp.max(peak, axis=-1, keepdims=True) * temper
            for j in range(3 * columns // 128):
                at = slice(j * 128, (j + 1) * 128)
                lifted = jnp.exp2(scores[p, :, at] * temper - top)
                shares[p, :, at] = lifted.astype(jnp.bfloat16)
            total = None
            for a in range(3):
                part = jnp.dot(
                    shares[p, :, a * columns : (a + 1) * columns],
                    values[p, row + a],
                    preferred_element_type=jnp.float32,
                )
                total = part if total is None else total + part
            blended.append((total[:, 0:channels] / total[:, channels:]).astype(jnp.bfloat16))
        message = jnp.dot(
            jnp.concatenate(blended, axis=1), out_w2[...], preferred_element_type=jnp.float32
        )
        scale = lax.rsqrt(jnp.mean(message * message, axis=-1, keepdims=True) + epsilon)
        out_ref[0, row] = state[row] + message * scale * message_gain_ref[...]
        return 0

    lax.fori_loop(0, rows, attend, 0)

    for side in range(2):
        halo_copy(0, side, halo_send_one, halo_recv_one).wait_send()
        halo_copy(1, side, halo_send_two, halo_recv_two).wait_send()
        edge_copy(side).wait_send()
    for g in range(4):
        for k in range(1, views):
            one_copy(g, k).wait_send()
            two_copy(g, k).wait_send()


def per_device(views, bands, features, tempers, partners, *weights):
    conv_one, conv_two, query_w, key_w, value_w, out_w, norm_gain, message_gain = weights
    _, rows, columns, channels = features.shape
    chunk = columns // views
    half = jnp.bfloat16
    full = jnp.float32
    any_space = pl.BlockSpec(memory_space=pl.ANY)
    vmem = pl.BlockSpec(memory_space=pltpu.VMEM)
    smem = pl.BlockSpec(memory_space=pltpu.SMEM)
    dma = pltpu.SemaphoreType.DMA
    line = (columns, channels)
    return pl.pallas_call(
        functools.partial(kernel, views, bands),
        out_shape=jax.ShapeDtypeStruct(features.shape, full),
        in_specs=[any_space, vmem, smem] + [vmem] * 8,
        out_specs=vmem,
        scratch_shapes=[
            pltpu.VMEM((rows,) + line, full),
            pltpu.VMEM((rows + 2, columns, 3 * channels), half),
            pltpu.VMEM((rows + 2, columns, 3 * channels), half),
            pltpu.VMEM((12 * channels, 2 * channels), half),
            pltpu.VMEM((12 * channels, 2 * channels), half),
            pltpu.VMEM((channels, 2 * channels), half),
            pltpu.VMEM((2 * channels, channels), half),
            pltpu.VMEM((2,) + line, half),
            pltpu.VMEM((2,) + line, half),
            pltpu.VMEM((2,) + line, half),
            pltpu.VMEM((2,) + line, half),
            pltpu.VMEM((rows,) + line, half),
            pltpu.VMEM((views, 2, chunk, channels), half),
            pltpu.VMEM((views, 2, chunk, channels), half),
            pltpu.VMEM((views, 2, chunk, channels), half),
            pltpu.VMEM((views, 2, chunk, channels), half),
            pltpu.VMEM((4, views, 2, 2, chunk, channels), half),
            pltpu.VMEM((2, rows + 2) + line, half),
            pltpu.VMEM((rows,) + line, half),
            pltpu.VMEM((2, rows + 2) + line, half),
            pltpu.VMEM((2, rows + 2, columns, 2 * channels), half),
            pltpu.VMEM((rows,) + line, full),
            pltpu.VMEM((2, columns, 3 * columns), full),
            pltpu.VMEM((2, columns, 3 * columns), half),
            dma((3,)),
            dma((2, 2)),
            dma((2, 2)),
            dma((4, views)),
            dma((4, views)),
            dma((4, views)),
            dma((4, views)),
            dma((2,)),
            dma((2,)),
        ],
        compiler_params=pltpu.CompilerParams(
            collective_id=0, has_side_effects=True, vmem_limit_bytes=60 * 1024 * 1024
        ),
    )(
        features,
        tempers,
        partners,
        conv_one,
        conv_two,
        query_w,
        key_w,
        value_w,
        out_w,
        norm_gain.reshape(1, channels),
        message_gain.reshape(1, channels),
    )


def solution(mesh):
    whole = P()
    in_specs = (
        P("view", "band", None, None),
        P("view", "band", None),
    ) + (whole,) * 9
    return jax.shard_map(
        functools.partial(per_device, mesh.shape["view"], mesh.shape["band"]),
        mesh=mesh,
        in_specs=in_specs,
        out_specs=P("view", "band", None, None),
        check_vma=False,
    )
```

```python
import functools
import math

import jax
import jax.numpy as jnp
from jax import lax
from jax.experimental import pallas as pl
from jax.experimental.pallas import tpu as pltpu
from jax.sharding import PartitionSpec as P

MESH = pl.DeviceIdType.MESH
epsilon = 1e-06
PAIR_STARTS = (2, 4, 0, 6)
ARRIVALS = (3, 4, 2, 5, 1, 0, 6, 7, 8, -1)
ATTENDED = (0, 0, 3, 4, 2, 1, 5, 6, 7, 0)


def kernel(
    views,
    bands,
    feat_ref,
    temper_ref,
    partners_ref,
    conv_one_ref,
    conv_two_ref,
    query_w_ref,
    key_w_ref,
    value_w_ref,
    out_w_ref,
    norm_gain_ref,
    message_gain_ref,
    out_ref,
    out_stage,
    state,
    taps_one,
    taps_two,
    kernel_one,
    kernel_two,
    query_w,
    kv_w,
    out_w2,
    halo_send_one,
    halo_recv_one,
    halo_send_two,
    halo_recv_two,
    normed,
    gather_a,
    gather_b,
    gather_c,
    gather_d,
    deal,
    pair,
    query,
    keys,
    values,
    temper_wide,
    scores,
    shares,
    load_sem,
    store_sem,
    halo_ssem,
    halo_rsem,
    one_ssem,
    one_rsem,
    two_ssem,
    two_rsem,
    edge_ssem,
    edge_rsem,
):
    rows, columns, channels = state.shape
    chunk = columns // views
    view = lax.axis_index("view")
    band = lax.axis_index("band")
    up = lax.rem(band + bands - 1, bands)
    down = lax.rem(band + 1, bands)
    strip = 32
    gathers = (gather_a, gather_b, gather_c, gather_d)

    def other(k):
        return lax.rem(view + k, views)

    barrier = pltpu.get_barrier_semaphore()
    for k in range(1, views):
        pl.semaphore_signal(barrier, inc=1, device_id={"view": other(k)}, device_id_type=MESH)
    for near in (up, down):
        pl.semaphore_signal(barrier, inc=1, device_id={"band": near}, device_id_type=MESH)
    routes = [
        (feat_ref.at[0, pl.ds(0, 1)], state.at[pl.ds(0, 1)]),
        (feat_ref.at[0, pl.ds(rows - 1, 1)], state.at[pl.ds(rows - 1, 1)]),
        (feat_ref.at[0, pl.ds(1, rows - 2)], state.at[pl.ds(1, rows - 2)]),
    ]
    for source, target in ((conv_one_ref, kernel_one), (conv_two_ref, kernel_two)):
        for a in range(3):
            for o in range(2):
                block = (pl.ds((a + o) * 3 * channels, 3 * channels), pl.ds(o * channels, channels))
                routes.append((source.at[a], target.at[block]))
    routes.append((key_w_ref, kv_w.at[:, pl.ds(0, channels)]))
    routes.append((value_w_ref, kv_w.at[:, pl.ds(channels, channels)]))
    routes.append((out_w_ref, out_w2.at[pl.ds(0, channels)]))
    routes.append((out_w_ref, out_w2.at[pl.ds(channels, channels)]))
    routes.append((query_w_ref, query_w))
    loads = [
        pltpu.make_async_copy(source, target, load_sem.at[i])
        for i, (source, target) in enumerate(routes)
    ]
    for load in loads:
        load.start()
    for target in (kernel_one, kernel_two):
        blank = jnp.zeros((3 * channels, channels), jnp.bfloat16)
        target[9 * channels : 12 * channels, 0:channels] = blank
        target[0 : 3 * channels, channels : 2 * channels] = blank

    def silu(x):
        half = 0.5 * x
        return half + half * jnp.tanh(half)

    place = lax.broadcasted_iota(jnp.int32, (columns, channels), 0)

    def store_taps(taps, row, x):
        before = jnp.where(place == 0, 0.0, pltpu.roll(x, 1, 0))
        after = jnp.where(place == columns - 1, 0.0, pltpu.roll(x, columns - 1, 0))
        taps[row, :, 0:channels] = before.astype(jnp.bfloat16)
        taps[row, :, channels : 2 * channels] = x.astype(jnp.bfloat16)
        taps[row, :, 2 * channels : 3 * channels] = after.astype(jnp.bfloat16)

    def halo_copy(stage, side, send, recv):
        return pltpu.make_async_remote_copy(
            src_ref=send.at[side],
            dst_ref=recv.at[side],
            send_sem=halo_ssem.at[stage, side],
            recv_sem=halo_rsem.at[stage, side],
            device_id={"band": down if side == 0 else up},
            device_id_type=MESH,
        )

    def edge_taps(taps, recv):
        above = recv[0].astype(jnp.float32)
        store_taps(taps, 0, jnp.where(band == 0, 0.0, above))
        below = recv[1].astype(jnp.float32)
        store_taps(taps, rows + 1, jnp.where(band == bands - 1, 0.0, below))

    def conv_pair(taps, weights, first):
        wide = jnp.concatenate([taps[first + i] for i in range(4)], axis=1)
        return jnp.dot(wide, weights[...], preferred_element_type=jnp.float32)

    loads[0].wait()
    loads[1].wait()
    for row, side in ((0, 1), (rows - 1, 0)):
        x = silu(state[row])
        halo_send_one[side] = x.astype(jnp.bfloat16)
        store_taps(taps_one, row + 1, x)
    pl.semaphore_wait(barrier, views + 1)
    for side in range(2):
        halo_copy(0, side, halo_send_one, halo_recv_one).start()

    loads[2].wait()

    def silu_row(row, _):
        store_taps(taps_one, row + 1, silu(state[row]))
        return 0

    lax.fori_loop(1, rows - 1, silu_row, 0)

    for load in loads[3:9]:
        load.wait()

    def finish_one(row, added):
        x = state[row] + added
        state[row] = x
        store_taps(taps_two, row + 1, silu(x))

    def conv_one_step(step, _):
        first = 1 + 2 * step
        added = conv_pair(taps_one, kernel_one, first)
        for o in range(2):
            finish_one(first + o, added[:, o * channels : (o + 1) * channels])
        return 0

    lax.fori_loop(0, rows // 2 - 1, conv_one_step, 0)

    def one_copy(g, k):
        first = PAIR_STARTS[g]
        return pltpu.make_async_remote_copy(
            src_ref=normed.at[pl.ds(first, 2), pl.ds(pl.multiple_of(other(k) * chunk, chunk), chunk)],
            dst_ref=gathers[g].at[view],
            send_sem=one_ssem.at[g, k],
            recv_sem=one_rsem.at[g, view],
            device_id={"view": other(k)},
            device_id_type=MESH,
        )

    def one_arrival(g, k):
        return pltpu.make_async_remote_copy(
            src_ref=gathers[g].at[other(k)],
            dst_ref=gathers[g].at[other(k)],
            send_sem=one_ssem.at[g, k],
            recv_sem=one_rsem.at[g, other(k)],
            device_id={"view": other(k)},
            device_id_type=MESH,
        )

    def conv_two_pair(first):
        added = conv_pair(taps_two, kernel_two, first)
        for o in range(2):
            x = state[first + o] + added[:, o * channels : (o + 1) * channels]
            state[first + o] = x
            scale = lax.rsqrt(jnp.mean(x * x, axis=-1, keepdims=True) + epsilon)
            normed[first + o] = (x * scale * norm_gain_ref[...]).astype(jnp.bfloat16)

    def scatter(g):
        for k in range(1, views):
            one_copy(g, k).start()

    for load in loads[9:15]:
        load.wait()

    def conv_two_inner(step, _):
        conv_two_pair(2 + 2 * step)
        for g in range(2):

            @pl.when(step == g)
            def _():
                scatter(g)

        return 0

    lax.fori_loop(0, 2, conv_two_inner, 0)

    for side in range(2):
        halo_copy(0, side, halo_send_one, halo_recv_one).wait_recv()
    edge_taps(taps_one, halo_recv_one)

    def conv_one_edge(step, _):
        row = (rows - 1) * step
        wide = jnp.concatenate([taps_one[row + i] for i in range(3)], axis=1)
        finish_one(
            row,
            jnp.dot(
                wide,
                kernel_one[0 : 9 * channels, 0:channels],
                preferred_element_type=jnp.float32,
            ),
        )
        return 0

    lax.fori_loop(0, 2, conv_one_edge, 0)
    halo_send_two[0] = taps_two[rows, :, channels : 2 * channels]
    halo_send_two[1] = taps_two[1, :, channels : 2 * channels]
    for side in range(2):
        halo_copy(1, side, halo_send_two, halo_recv_two).start()

    for load in loads[15:]:
        load.wait()
    factor = 1.0 / math.sqrt(channels) * math.log2(math.e)
    for c in range(columns // 128):
        at = slice(c * 128, (c + 1) * 128)
        turned = jnp.concatenate([temper_ref[0, :, at] * factor] * (128 // rows), axis=0).T
        for row in range(rows):
            temper_wide[row, at, :] = jnp.broadcast_to(turned[:, row : row + 1], (128, channels))

    def fill_ones(row, _):
        for p in range(2):
            at = pl.ds(pl.multiple_of(row * columns, columns), columns)
            values[p, at, channels : 2 * channels] = jnp.ones((columns, channels), jnp.bfloat16)
        return 0

    lax.fori_loop(0, rows + 2, fill_ones, 0)

    own = pl.ds(pl.multiple_of(view * chunk, chunk), chunk)

    def two_copy(row, k):
        return pltpu.make_async_remote_copy(
            src_ref=deal.at[row, k],
            dst_ref=pair.at[:, row + 1, own],
            send_sem=two_ssem.at[row, k],
            recv_sem=two_rsem.at[row, view],
            device_id={"view": other(k)},
            device_id_type=MESH,
        )

    def two_arrival(row, k):
        theirs = pl.ds(pl.multiple_of(other(k) * chunk, chunk), chunk)
        return pltpu.make_async_remote_copy(
            src_ref=deal.at[row, k],
            dst_ref=pair.at[:, row + 1, theirs],
            send_sem=two_ssem.at[row, k],
            recv_sem=two_rsem.at[row, other(k)],
            device_id={"view": other(k)},
            device_id_type=MESH,
        )

    def gathered(g):
        gathers[g][view] = normed[pl.ds(PAIR_STARTS[g], 2), own]
        for k in range(1, views):
            one_arrival(g, k).wait_recv()

    def deal_row(row):
        g = PAIR_STARTS.index(row - row % 2)
        for k in range(1, views):
            for p in range(2):
                deal[row, k, p] = gathers[g][partners_ref[p, other(k)], row % 2]
        for p in range(2):
            pair[p, row + 1, own] = gathers[g][partners_ref[p, view], row % 2]
        for k in range(1, views):
            two_copy(row, k).start()

    gathered(0)
    deal_row(3)

    for side in range(2):
        halo_copy(1, side, halo_send_two, halo_recv_two).wait_recv()
    edge_taps(taps_two, halo_recv_two)

    def conv_two_edge(step, _):
        conv_two_pair((rows - 2) * step)
        return 0

    lax.fori_loop(0, 2, conv_two_edge, 0)

    gathered(1)
    deal_row(4)
    deal_row(2)
    scatter(2)
    deal_row(5)
    scatter(3)

    def query_row(row, _):
        query[row] = jnp.dot(
            normed[row], query_w[...], preferred_element_type=jnp.float32
        ).astype(jnp.bfloat16)
        return 0

    lax.fori_loop(0, rows, query_row, 0)

    def edge_copy(side):
        source, target = ((rows, 0), (1, rows + 1))[side]
        return pltpu.make_async_remote_copy(
            src_ref=pair.at[:, source],
            dst_ref=pair.at[:, target],
            send_sem=edge_ssem.at[side],
            recv_sem=edge_rsem.at[side],
            device_id={"band": down if side == 0 else up},
            device_id_type=MESH,
        )

    def pick(table, step):
        packed = sum(entry << (4 * n) for n, entry in enumerate(table[:7]))
        rest = sum(entry << (4 * n) for n, entry in enumerate(table[7:]))
        late = step // 7
        word = (1 - late) * packed + late * rest
        return lax.shift_right_logical(word, 4 * (step - 7 * late)) % 16

    def store_out(row):
        return pltpu.make_async_copy(out_stage.at[row], out_ref.at[0, row], store_sem.at[row])

    def attend(step, _):
        row = pick(ATTENDED, step)
        place_in = pick([r + 1 for r in ARRIVALS], step)
        for n, r in enumerate(ARRIVALS):

            @pl.when(step == n)
            def _(n=n, r=r):
                if n == 3:
                    gathered(2)
                    deal_row(1)
                    deal_row(0)
                if n == 4:
                    gathered(3)
                    deal_row(6)
                    deal_row(7)
                if 0 <= r < rows:
                    for k in range(1, views):
                        two_arrival(r, k).wait_recv()
                    if r == 0:
                        edge_copy(1).start()
                    if r == rows - 1:
                        edge_copy(0).start()
                else:
                    side = 1 if r == rows else 0
                    edge_copy(side).wait_recv()
                    outside = (band == bands - 1) if side == 1 else (band == 0)

                    @pl.when(outside)
                    def _():
                        pair[:, r + 1] = jnp.zeros((2, columns, channels), jnp.bfloat16)

        for p in range(2):
            both = jnp.dot(pair[p, place_in], kv_w[...], preferred_element_type=jnp.float32)
            both = both.astype(jnp.bfloat16)
            at = pl.ds(pl.multiple_of(place_in * columns, columns), columns)
            keys[p, at] = both[:, 0:channels]
            values[p, at, 0:channels] = both[:, channels : 2 * channels]

        @pl.when(step >= 2)
        def _():
            attend_row(row)
            store_out(row).start()

        return 0

    def attend_row(row):
        blended = []
        window = pl.ds(pl.multiple_of(row * columns, columns), 3 * columns)
        for p in range(2):
            scores[p] = lax.dot_general(
                query[row],
                keys[p, window],
                (((1,), (1,)), ((), ())),
                preferred_element_type=jnp.float32,
            )
        for p in range(2):
            for k in range(columns // strip):
                at = slice(k * strip, (k + 1) * strip)
                temper = temper_wide[row, at]
                lanes = range(3 * columns // 128)
                parts = [scores[p, at, j * 128 : (j + 1) * 128] for j in lanes]
                peak = functools.reduce(jnp.maximum, parts)
                top = jnp.max(peak, axis=-1, keepdims=True) * temper
                for j in lanes:
                    lifted = jnp.exp2(parts[j] * temper - top)
                    shares[p, at, j * 128 : (j + 1) * 128] = lifted.astype(jnp.bfloat16)
            total = jnp.dot(shares[p], values[p, window], preferred_element_type=jnp.float32)
            blended.append((total[:, 0:channels] / total[:, channels:]).astype(jnp.bfloat16))
        message = jnp.dot(
            jnp.concatenate(blended, axis=1), out_w2[...], preferred_element_type=jnp.float32
        )
        scale = lax.rsqrt(jnp.mean(message * message, axis=-1, keepdims=True) + epsilon)
        out_stage[row] = state[row] + message * scale * message_gain_ref[...]

    lax.fori_loop(0, rows + 2, attend, 0)

    for side in range(2):
        halo_copy(0, side, halo_send_one, halo_recv_one).wait_send()
        halo_copy(1, side, halo_send_two, halo_recv_two).wait_send()
        edge_copy(side).wait_send()
    for g in range(4):
        for k in range(1, views):
            one_copy(g, k).wait_send()
    for row in range(rows):
        store_out(row).wait()
        for k in range(1, views):
            two_copy(row, k).wait_send()


def per_device(views, bands, features, tempers, partners, *weights):
    conv_one, conv_two, query_w, key_w, value_w, out_w, norm_gain, message_gain = weights
    _, rows, columns, channels = features.shape
    chunk = columns // views
    half = jnp.bfloat16
    full = jnp.float32
    any_space = pl.BlockSpec(memory_space=pl.ANY)
    vmem = pl.BlockSpec(memory_space=pltpu.VMEM)
    smem = pl.BlockSpec(memory_space=pltpu.SMEM)
    dma = pltpu.SemaphoreType.DMA
    line = (columns, channels)
    return pl.pallas_call(
        functools.partial(kernel, views, bands),
        out_shape=jax.ShapeDtypeStruct(features.shape, full),
        in_specs=[any_space, vmem, smem] + [any_space] * 6 + [vmem] * 2,
        out_specs=any_space,
        scratch_shapes=[
            pltpu.VMEM((rows,) + line, full),
            pltpu.VMEM((rows,) + line, full),
            pltpu.VMEM((rows + 2, columns, 3 * channels), half),
            pltpu.VMEM((rows + 2, columns, 3 * channels), half),
            pltpu.VMEM((12 * channels, 2 * channels), half),
            pltpu.VMEM((12 * channels, 2 * channels), half),
            pltpu.VMEM((channels, channels), half),
            pltpu.VMEM((channels, 2 * channels), half),
            pltpu.VMEM((2 * channels, channels), half),
            pltpu.VMEM((2,) + line, half),
            pltpu.VMEM((2,) + line, half),
            pltpu.VMEM((2,) + line, half),
            pltpu.VMEM((2,) + line, half),
            pltpu.VMEM((rows,) + line, half),
            pltpu.VMEM((views, 2, chunk, channels), half),
            pltpu.VMEM((views, 2, chunk, channels), half),
            pltpu.VMEM((views, 2, chunk, channels), half),
            pltpu.VMEM((views, 2, chunk, channels), half),
            pltpu.VMEM((rows, views, 2, chunk, channels), half),
            pltpu.VMEM((2, rows + 2) + line, half),
            pltpu.VMEM((rows,) + line, half),
            pltpu.VMEM((2, (rows + 2) * columns, channels), half),
            pltpu.VMEM((2, (rows + 2) * columns, 2 * channels), half),
            pltpu.VMEM((rows,) + line, full),
            pltpu.VMEM((2, columns, 3 * columns), full),
            pltpu.VMEM((2, columns, 3 * columns), half),
            dma((20,)),
            dma((rows,)),
            dma((2, 2)),
            dma((2, 2)),
            dma((4, views)),
            dma((4, views)),
            dma((rows, views)),
            dma((rows, views)),
            dma((2,)),
            dma((2,)),
        ],
        compiler_params=pltpu.CompilerParams(
            collective_id=0, has_side_effects=True, vmem_limit_bytes=60 * 1024 * 1024
        ),
    )(
        features,
        tempers,
        partners.T,
        conv_one.reshape(3, 3 * channels, channels),
        conv_two.reshape(3, 3 * channels, channels),
        query_w,
        key_w,
        value_w,
        out_w,
        norm_gain.reshape(1, channels),
        message_gain.reshape(1, channels),
    )


def solution(mesh):
    whole = P()
    in_specs = (
        P("view", "band", None, None),
        P("view", "band", None),
    ) + (whole,) * 9
    return jax.shard_map(
        functools.partial(per_device, mesh.shape["view"], mesh.shape["band"]),
        mesh=mesh,
        in_specs=in_specs,
        out_specs=P("view", "band", None, None),
        check_vma=False,
    )
```

```python
import functools
import math

import jax
import jax.numpy as jnp
from jax import lax
from jax.experimental import pallas as pl
from jax.experimental.pallas import tpu as pltpu
from jax.sharding import PartitionSpec as P

MESH = pl.DeviceIdType.MESH
epsilon = 1e-06
PAIR_STARTS = (2, 4, 0, 6)
ARRIVALS = (3, 4, 2, 5, 1, 0, 6, 7, 8, -1)
ATTENDED = (0, 0, 3, 4, 2, 1, 5, 6, 7, 0)


def kernel(
    views,
    bands,
    feat_ref,
    temper_ref,
    partners_ref,
    conv_one_ref,
    conv_two_ref,
    query_w_ref,
    key_w_ref,
    value_w_ref,
    out_w_ref,
    norm_gain_ref,
    message_gain_ref,
    out_ref,
    temper_in,
    partners_in,
    gains,
    out_stage,
    state,
    taps_one,
    taps_two,
    kernel_one,
    kernel_two,
    query_w,
    kv_w,
    out_w2,
    halo_send_one,
    halo_recv_one,
    halo_send_two,
    halo_recv_two,
    normed,
    gather_a,
    gather_b,
    gather_c,
    gather_d,
    deal,
    pair,
    query,
    keys,
    values,
    temper_wide,
    scores,
    shares,
    load_sem,
    store_sem,
    halo_ssem,
    halo_rsem,
    one_ssem,
    one_rsem,
    two_ssem,
    two_rsem,
    edge_ssem,
    edge_rsem,
):
    rows, columns, channels = state.shape
    chunk = columns // views
    view = lax.axis_index("view")
    band = lax.axis_index("band")
    up = lax.rem(band + bands - 1, bands)
    down = lax.rem(band + 1, bands)
    strip = 32
    gathers = (gather_a, gather_b, gather_c, gather_d)

    def other(k):
        return lax.rem(view + k, views)

    barrier = pltpu.get_barrier_semaphore()
    for k in range(1, views):
        pl.semaphore_signal(barrier, inc=1, device_id={"view": other(k)}, device_id_type=MESH)
    for near in (up, down):
        pl.semaphore_signal(barrier, inc=1, device_id={"band": near}, device_id_type=MESH)
    routes = [
        (feat_ref.at[0, pl.ds(0, 1)], state.at[pl.ds(0, 1)]),
        (feat_ref.at[0, pl.ds(rows - 1, 1)], state.at[pl.ds(rows - 1, 1)]),
        (feat_ref.at[0, pl.ds(1, rows - 2)], state.at[pl.ds(1, rows - 2)]),
    ]
    for source, target in ((conv_one_ref, kernel_one), (conv_two_ref, kernel_two)):
        for a in range(3):
            for o in range(2):
                block = (pl.ds((a + o) * 3 * channels, 3 * channels), pl.ds(o * channels, channels))
                routes.append((source.at[a], target.at[block]))
    routes.append((key_w_ref, kv_w.at[:, pl.ds(0, channels)]))
    routes.append((value_w_ref, kv_w.at[:, pl.ds(channels, channels)]))
    routes.append((out_w_ref, out_w2.at[pl.ds(0, channels)]))
    routes.append((out_w_ref, out_w2.at[pl.ds(channels, channels)]))
    routes.append((query_w_ref, query_w))
    routes.append((temper_ref.at[0], temper_in))
    routes.append((partners_ref, partners_in))
    routes.append((norm_gain_ref, gains.at[0]))
    routes.append((message_gain_ref, gains.at[1]))
    loads = [
        pltpu.make_async_copy(source, target, load_sem.at[i])
        for i, (source, target) in enumerate(routes)
    ]
    for load in loads:
        load.start()
    for target in (kernel_one, kernel_two):
        blank = jnp.zeros((3 * channels, channels), jnp.bfloat16)
        target[9 * channels : 12 * channels, 0:channels] = blank
        target[0 : 3 * channels, channels : 2 * channels] = blank

    def silu(x):
        half = 0.5 * x
        return half + half * jnp.tanh(half)

    place = lax.broadcasted_iota(jnp.int32, (columns, channels), 0)

    def store_taps(taps, row, x):
        before = jnp.where(place == 0, 0.0, pltpu.roll(x, 1, 0))
        after = jnp.where(place == columns - 1, 0.0, pltpu.roll(x, columns - 1, 0))
        taps[row, :, 0:channels] = before.astype(jnp.bfloat16)
        taps[row, :, channels : 2 * channels] = x.astype(jnp.bfloat16)
        taps[row, :, 2 * channels : 3 * channels] = after.astype(jnp.bfloat16)

    def halo_copy(stage, side, send, recv):
        return pltpu.make_async_remote_copy(
            src_ref=send.at[side],
            dst_ref=recv.at[side],
            send_sem=halo_ssem.at[stage, side],
            recv_sem=halo_rsem.at[stage, side],
            device_id={"band": down if side == 0 else up},
            device_id_type=MESH,
        )

    def edge_taps(taps, recv):
        above = recv[0].astype(jnp.float32)
        store_taps(taps, 0, jnp.where(band == 0, 0.0, above))
        below = recv[1].astype(jnp.float32)
        store_taps(taps, rows + 1, jnp.where(band == bands - 1, 0.0, below))

    def conv_pair(taps, weights, first):
        wide = jnp.concatenate([taps[first + i] for i in range(4)], axis=1)
        return jnp.dot(wide, weights[...], preferred_element_type=jnp.float32)

    loads[0].wait()
    loads[1].wait()
    for row, side in ((0, 1), (rows - 1, 0)):
        x = silu(state[row])
        halo_send_one[side] = x.astype(jnp.bfloat16)
        store_taps(taps_one, row + 1, x)
    loads[2].wait()

    def silu_row(row, _):
        store_taps(taps_one, row + 1, silu(state[row]))
        return 0

    lax.fori_loop(1, rows - 1, silu_row, 0)

    for load in loads[3:9]:
        load.wait()

    def finish_one(row, added):
        x = state[row] + added
        state[row] = x
        store_taps(taps_two, row + 1, silu(x))

    def conv_one_step(step, _):
        first = 1 + 2 * step
        added = conv_pair(taps_one, kernel_one, first)
        for o in range(2):
            finish_one(first + o, added[:, o * channels : (o + 1) * channels])
        return 0

    lax.fori_loop(0, rows // 2 - 1, conv_one_step, 0)

    def one_copy(g, k):
        first = PAIR_STARTS[g]
        return pltpu.make_async_remote_copy(
            src_ref=normed.at[pl.ds(first, 2), pl.ds(pl.multiple_of(other(k) * chunk, chunk), chunk)],
            dst_ref=gathers[g].at[view],
            send_sem=one_ssem.at[g, k],
            recv_sem=one_rsem.at[g, view],
            device_id={"view": other(k)},
            device_id_type=MESH,
        )

    def one_arrival(g, k):
        return pltpu.make_async_remote_copy(
            src_ref=gathers[g].at[other(k)],
            dst_ref=gathers[g].at[other(k)],
            send_sem=one_ssem.at[g, k],
            recv_sem=one_rsem.at[g, other(k)],
            device_id={"view": other(k)},
            device_id_type=MESH,
        )

    def conv_two_pair(first):
        added = conv_pair(taps_two, kernel_two, first)
        for o in range(2):
            x = state[first + o] + added[:, o * channels : (o + 1) * channels]
            state[first + o] = x
            scale = lax.rsqrt(jnp.mean(x * x, axis=-1, keepdims=True) + epsilon)
            normed[first + o] = (x * scale * gains[0]).astype(jnp.bfloat16)

    def scatter(g):
        for k in range(1, views):
            one_copy(g, k).start()

    loads[22].wait()
    for load in loads[9:15]:
        load.wait()

    def conv_two_inner(step, _):
        conv_two_pair(2 + 2 * step)
        for g in range(2):

            @pl.when(step == g)
            def _():
                if g == 0:
                    pl.semaphore_wait(barrier, views + 1)
                    for side in range(2):
                        halo_copy(0, side, halo_send_one, halo_recv_one).start()
                scatter(g)

        return 0

    lax.fori_loop(0, 2, conv_two_inner, 0)

    for load in loads[15:22] + loads[23:]:
        load.wait()
    factor = 1.0 / math.sqrt(channels) * math.log2(math.e)
    for c in range(columns // 128):
        at = slice(c * 128, (c + 1) * 128)
        turned = jnp.concatenate([temper_in[:, at] * factor] * (128 // rows), axis=0).T
        for row in range(rows):
            temper_wide[row, at, :] = jnp.broadcast_to(turned[:, row : row + 1], (128, channels))

    def fill_ones(row, _):
        for p in range(2):
            at = pl.ds(pl.multiple_of(row * columns, columns), columns)
            values[p, at, channels : 2 * channels] = jnp.ones((columns, channels), jnp.bfloat16)
        return 0

    lax.fori_loop(0, rows + 2, fill_ones, 0)

    own = pl.ds(pl.multiple_of(view * chunk, chunk), chunk)

    def two_copy(row, k):
        return pltpu.make_async_remote_copy(
            src_ref=deal.at[row, k],
            dst_ref=pair.at[:, row + 1, own],
            send_sem=two_ssem.at[row, k],
            recv_sem=two_rsem.at[row, view],
            device_id={"view": other(k)},
            device_id_type=MESH,
        )

    def two_arrival(row, k):
        theirs = pl.ds(pl.multiple_of(other(k) * chunk, chunk), chunk)
        return pltpu.make_async_remote_copy(
            src_ref=deal.at[row, k],
            dst_ref=pair.at[:, row + 1, theirs],
            send_sem=two_ssem.at[row, k],
            recv_sem=two_rsem.at[row, other(k)],
            device_id={"view": other(k)},
            device_id_type=MESH,
        )

    def gathered(g):
        gathers[g][view] = normed[pl.ds(PAIR_STARTS[g], 2), own]
        for k in range(1, views):
            one_arrival(g, k).wait_recv()

    def deal_row(row):
        g = PAIR_STARTS.index(row - row % 2)
        for k in range(1, views):
            for p in range(2):
                deal[row, k, p] = gathers[g][partners_in[p, other(k)], row % 2]
        for p in range(2):
            pair[p, row + 1, own] = gathers[g][partners_in[p, view], row % 2]
        for k in range(1, views):
            two_copy(row, k).start()

    gathered(0)
    deal_row(3)
    gathered(1)
    deal_row(4)
    deal_row(2)
    deal_row(5)

    for side in range(2):
        halo_copy(0, side, halo_send_one, halo_recv_one).wait_recv()
    edge_taps(taps_one, halo_recv_one)

    def conv_one_edge(step, _):
        row = (rows - 1) * step
        wide = jnp.concatenate([taps_one[row + i] for i in range(3)], axis=1)
        finish_one(
            row,
            jnp.dot(
                wide,
                kernel_one[0 : 9 * channels, 0:channels],
                preferred_element_type=jnp.float32,
            ),
        )
        return 0

    lax.fori_loop(0, 2, conv_one_edge, 0)
    halo_send_two[0] = taps_two[rows, :, channels : 2 * channels]
    halo_send_two[1] = taps_two[1, :, channels : 2 * channels]
    for side in range(2):
        halo_copy(1, side, halo_send_two, halo_recv_two).start()

    def query_row(row, _):
        query[row] = jnp.dot(
            normed[row], query_w[...], preferred_element_type=jnp.float32
        ).astype(jnp.bfloat16)
        return 0

    lax.fori_loop(2, rows - 2, query_row, 0)

    for side in range(2):
        halo_copy(1, side, halo_send_two, halo_recv_two).wait_recv()
    edge_taps(taps_two, halo_recv_two)

    def conv_two_edge(step, _):
        conv_two_pair((rows - 2) * step)
        return 0

    lax.fori_loop(0, 2, conv_two_edge, 0)

    scatter(2)
    scatter(3)
    lax.fori_loop(0, 2, query_row, 0)
    lax.fori_loop(rows - 2, rows, query_row, 0)

    def edge_copy(side, k):
        source, target = ((rows, 0), (1, rows + 1))[side]
        at = pl.ds(pl.multiple_of(other(k) * chunk, chunk), chunk)
        return pltpu.make_async_remote_copy(
            src_ref=pair.at[:, source, at],
            dst_ref=pair.at[:, target, at],
            send_sem=edge_ssem.at[side, k],
            recv_sem=edge_rsem.at[side, k],
            device_id={"band": down if side == 0 else up},
            device_id_type=MESH,
        )

    def pick(table, step):
        packed = sum(entry << (4 * n) for n, entry in enumerate(table[:7]))
        rest = sum(entry << (4 * n) for n, entry in enumerate(table[7:]))
        late = step // 7
        word = (1 - late) * packed + late * rest
        return lax.shift_right_logical(word, 4 * (step - 7 * late)) % 16

    def store_out(row):
        return pltpu.make_async_copy(out_stage.at[row], out_ref.at[0, row], store_sem.at[row])

    def attend(step, _):
        row = pick(ATTENDED, step)
        place_in = pick([r + 1 for r in ARRIVALS], step)
        for n, r in enumerate(ARRIVALS):

            @pl.when(step == n)
            def _(n=n, r=r):
                if n == 3:
                    gathered(2)
                    deal_row(1)
                    deal_row(0)
                if n == 4:
                    gathered(3)
                    deal_row(6)
                    deal_row(7)
                if 0 <= r < rows:
                    side = {0: 1, rows - 1: 0}.get(r)
                    if side is not None:
                        edge_copy(side, 0).start()
                    for k in range(1, views):
                        two_arrival(r, k).wait_recv()
                        if side is not None:
                            edge_copy(side, k).start()
                else:
                    side = 1 if r == rows else 0
                    for k in range(views):
                        edge_copy(side, k).wait_recv()
                    outside = (band == bands - 1) if side == 1 else (band == 0)

                    @pl.when(outside)
                    def _():
                        pair[:, r + 1] = jnp.zeros((2, columns, channels), jnp.bfloat16)

        for p in range(2):
            both = jnp.dot(pair[p, place_in], kv_w[...], preferred_element_type=jnp.float32)
            both = both.astype(jnp.bfloat16)
            at = pl.ds(pl.multiple_of(place_in * columns, columns), columns)
            keys[p, at] = both[:, 0:channels]
            values[p, at, 0:channels] = both[:, channels : 2 * channels]

        @pl.when(step >= 2)
        def _():
            attend_row(row)
            store_out(row).start()

        return 0

    def attend_row(row):
        blended = []
        window = pl.ds(pl.multiple_of(row * columns, columns), 3 * columns)
        for p in range(2):
            scores[p] = lax.dot_general(
                query[row],
                keys[p, window],
                (((1,), (1,)), ((), ())),
                preferred_element_type=jnp.float32,
            )
        for p in range(2):
            for k in range(columns // strip):
                at = slice(k * strip, (k + 1) * strip)
                temper = temper_wide[row, at]
                lanes = range(3 * columns // 128)
                parts = [scores[p, at, j * 128 : (j + 1) * 128] for j in lanes]
                peak = functools.reduce(jnp.maximum, parts)
                top = jnp.max(peak, axis=-1, keepdims=True) * temper
                for j in lanes:
                    lifted = jnp.exp2(parts[j] * temper - top)
                    shares[p, at, j * 128 : (j + 1) * 128] = lifted.astype(jnp.bfloat16)
            total = jnp.dot(shares[p], values[p, window], preferred_element_type=jnp.float32)
            blended.append((total[:, 0:channels] / total[:, channels:]).astype(jnp.bfloat16))
        message = jnp.dot(
            jnp.concatenate(blended, axis=1), out_w2[...], preferred_element_type=jnp.float32
        )
        scale = lax.rsqrt(jnp.mean(message * message, axis=-1, keepdims=True) + epsilon)
        out_stage[row] = state[row] + message * scale * gains[1]

    lax.fori_loop(0, rows + 2, attend, 0)

    for side in range(2):
        halo_copy(0, side, halo_send_one, halo_recv_one).wait_send()
        halo_copy(1, side, halo_send_two, halo_recv_two).wait_send()
        for k in range(views):
            edge_copy(side, k).wait_send()
    for g in range(4):
        for k in range(1, views):
            one_copy(g, k).wait_send()
    for row in range(rows):
        store_out(row).wait()
        for k in range(1, views):
            two_copy(row, k).wait_send()


def hand_over(source, target, stage, in_sem, out_sem):
    count = stage.shape[0]
    reads = [
        pltpu.make_async_copy(source.at[0, i], stage.at[i], in_sem.at[i]) for i in range(count)
    ]
    writes = [
        pltpu.make_async_copy(stage.at[i], target.at[0, i], out_sem.at[i]) for i in range(count)
    ]
    for read in reads:
        read.start()
    for read, write in zip(reads, writes):
        read.wait()
        write.start()
    for write in writes:
        write.wait()


def per_device(views, bands, features, tempers, partners, *weights):
    conv_one, conv_two, query_w, key_w, value_w, out_w, norm_gain, message_gain = weights
    _, rows, columns, channels = features.shape
    chunk = columns // views
    half = jnp.bfloat16
    full = jnp.float32
    any_space = pl.BlockSpec(memory_space=pl.ANY)
    dma = pltpu.SemaphoreType.DMA
    line = (columns, channels)
    refined = pl.pallas_call(
        functools.partial(kernel, views, bands),
        out_shape=jax.ShapeDtypeStruct(features.shape, full),
        in_specs=[any_space] * 11,
        out_specs=any_space,
        scratch_shapes=[
            pltpu.VMEM((rows, columns), full),
            pltpu.SMEM((2, views), jnp.int32),
            pltpu.VMEM((2, 1, channels), full),
            pltpu.VMEM((rows,) + line, full),
            pltpu.VMEM((rows,) + line, full),
            pltpu.VMEM((rows + 2, columns, 3 * channels), half),
            pltpu.VMEM((rows + 2, columns, 3 * channels), half),
            pltpu.VMEM((12 * channels, 2 * channels), half),
            pltpu.VMEM((12 * channels, 2 * channels), half),
            pltpu.VMEM((channels, channels), half),
            pltpu.VMEM((channels, 2 * channels), half),
            pltpu.VMEM((2 * channels, channels), half),
            pltpu.VMEM((2,) + line, half),
            pltpu.VMEM((2,) + line, half),
            pltpu.VMEM((2,) + line, half),
            pltpu.VMEM((2,) + line, half),
            pltpu.VMEM((rows,) + line, half),
            pltpu.VMEM((views, 2, chunk, channels), half),
            pltpu.VMEM((views, 2, chunk, channels), half),
            pltpu.VMEM((views, 2, chunk, channels), half),
            pltpu.VMEM((views, 2, chunk, channels), half),
            pltpu.VMEM((rows, views, 2, chunk, channels), half),
            pltpu.VMEM((2, rows + 2) + line, half),
            pltpu.VMEM((rows,) + line, half),
            pltpu.VMEM((2, (rows + 2) * columns, channels), half),
            pltpu.VMEM((2, (rows + 2) * columns, 2 * channels), half),
            pltpu.VMEM((rows,) + line, full),
            pltpu.VMEM((2, columns, 3 * columns), full),
            pltpu.VMEM((2, columns, 3 * columns), half),
            dma((24,)),
            dma((rows,)),
            dma((2, 2)),
            dma((2, 2)),
            dma((4, views)),
            dma((4, views)),
            dma((rows, views)),
            dma((rows, views)),
            dma((2, views)),
            dma((2, views)),
        ],
        compiler_params=pltpu.CompilerParams(
            collective_id=0, has_side_effects=True, vmem_limit_bytes=60 * 1024 * 1024
        ),
    )(
        features,
        tempers,
        partners.T,
        conv_one.reshape(3, 3 * channels, channels),
        conv_two.reshape(3, 3 * channels, channels),
        query_w,
        key_w,
        value_w,
        out_w,
        norm_gain.reshape(1, channels),
        message_gain.reshape(1, channels),
    )
    return pl.pallas_call(
        hand_over,
        out_shape=jax.ShapeDtypeStruct(features.shape, full),
        in_specs=[any_space],
        out_specs=any_space,
        scratch_shapes=[pltpu.VMEM((rows,) + line, full), dma((rows,)), dma((rows,))],
        compiler_params=pltpu.CompilerParams(vmem_limit_bytes=60 * 1024 * 1024),
    )(refined)


def solution(mesh):
    whole = P()
    in_specs = (
        P("view", "band", None, None),
        P("view", "band", None),
    ) + (whole,) * 9
    return jax.shard_map(
        functools.partial(per_device, mesh.shape["view"], mesh.shape["band"]),
        mesh=mesh,
        in_specs=in_specs,
        out_specs=P("view", "band", None, None),
        check_vma=False,
    )
```

```python
import functools
import math

import jax
import jax.numpy as jnp
from jax import lax
from jax.experimental import pallas as pl
from jax.experimental.pallas import tpu as pltpu
from jax.sharding import PartitionSpec as P

MESH = pl.DeviceIdType.MESH
epsilon = 1e-06
PAIR_STARTS = (2, 4, 0, 6)
ARRIVALS = (3, 4, 2, 5, 1, 0, 6, 7, 8, -1)
ATTENDED = (0, 0, 3, 4, 2, 1, 5, 6, 7, 0)


def kernel(
    views,
    bands,
    feat_ref,
    temper_ref,
    partners_ref,
    conv_one_ref,
    conv_two_ref,
    query_w_ref,
    key_w_ref,
    value_w_ref,
    out_w_ref,
    norm_gain_ref,
    message_gain_ref,
    out_ref,
    temper_in,
    partners_in,
    gains,
    out_stage,
    state,
    taps_one,
    taps_two,
    kernel_one,
    kernel_two,
    query_w,
    kv_w,
    out_w2,
    halo_send_one,
    halo_recv_one,
    halo_send_two,
    halo_recv_two,
    normed,
    gather_a,
    gather_b,
    gather_c,
    gather_d,
    deal,
    pair,
    query,
    keys,
    values,
    temper_wide,
    scores,
    shares,
    load_sem,
    store_sem,
    halo_ssem,
    halo_rsem,
    one_ssem,
    one_rsem,
    two_ssem,
    two_rsem,
    edge_ssem,
    edge_rsem,
):
    rows, columns, channels = state.shape
    chunk = columns // views
    view = lax.axis_index("view")
    band = lax.axis_index("band")
    up = lax.rem(band + bands - 1, bands)
    down = lax.rem(band + 1, bands)
    strip = 32
    gathers = (gather_a, gather_b, gather_c, gather_d)
    leaves = (band < bands - 1, band > 0)
    enters = (band > 0, band < bands - 1)

    def other(k):
        return lax.rem(view + k, views)

    barrier = pltpu.get_barrier_semaphore()
    for k in range(1, views):
        pl.semaphore_signal(barrier, inc=1, device_id={"view": other(k)}, device_id_type=MESH)
    for near in (up, down):
        pl.semaphore_signal(barrier, inc=1, device_id={"band": near}, device_id_type=MESH)
    routes = [
        (feat_ref.at[0, pl.ds(0, 1)], state.at[pl.ds(0, 1)]),
        (feat_ref.at[0, pl.ds(rows - 1, 1)], state.at[pl.ds(rows - 1, 1)]),
        (feat_ref.at[0, pl.ds(1, rows - 2)], state.at[pl.ds(1, rows - 2)]),
    ]
    for source, target in ((conv_one_ref, kernel_one), (conv_two_ref, kernel_two)):
        for a in range(3):
            for o in range(2):
                block = (pl.ds((a + o) * 3 * channels, 3 * channels), pl.ds(o * channels, channels))
                routes.append((source.at[a], target.at[block]))
    routes.append((key_w_ref, kv_w.at[:, pl.ds(0, channels)]))
    routes.append((value_w_ref, kv_w.at[:, pl.ds(channels, channels)]))
    routes.append((out_w_ref, out_w2.at[pl.ds(0, channels)]))
    routes.append((out_w_ref, out_w2.at[pl.ds(channels, channels)]))
    routes.append((query_w_ref, query_w))
    routes.append((temper_ref.at[0], temper_in))
    routes.append((partners_ref, partners_in))
    routes.append((norm_gain_ref, gains.at[0]))
    routes.append((message_gain_ref, gains.at[1]))
    loads = [
        pltpu.make_async_copy(source, target, load_sem.at[i])
        for i, (source, target) in enumerate(routes)
    ]
    for load in loads:
        load.start()
    for target in (kernel_one, kernel_two):
        blank = jnp.zeros((3 * channels, channels), jnp.bfloat16)
        target[9 * channels : 12 * channels, 0:channels] = blank
        target[0 : 3 * channels, channels : 2 * channels] = blank

    def silu(x):
        half = 0.5 * x
        return half + half * jnp.tanh(half)

    place = lax.broadcasted_iota(jnp.int32, (columns, channels), 0)

    def store_taps(taps, row, x):
        before = jnp.where(place == 0, 0.0, pltpu.roll(x, 1, 0))
        after = jnp.where(place == columns - 1, 0.0, pltpu.roll(x, columns - 1, 0))
        taps[row, :, 0:channels] = before.astype(jnp.bfloat16)
        taps[row, :, channels : 2 * channels] = x.astype(jnp.bfloat16)
        taps[row, :, 2 * channels : 3 * channels] = after.astype(jnp.bfloat16)

    def halo_copy(stage, side, send, recv):
        return pltpu.make_async_remote_copy(
            src_ref=send.at[side],
            dst_ref=recv.at[side],
            send_sem=halo_ssem.at[stage, side],
            recv_sem=halo_rsem.at[stage, side],
            device_id={"band": down if side == 0 else up},
            device_id_type=MESH,
        )

    def edge_taps(taps, recv):
        for side, row in ((0, 0), (1, rows + 1)):

            @pl.when(jnp.logical_not(enters[side]))
            def _():
                recv[side] = jnp.zeros((columns, channels), jnp.bfloat16)

            store_taps(taps, row, recv[side].astype(jnp.float32))

    def conv_pair(taps, weights, first):
        wide = jnp.concatenate([taps[first + i] for i in range(4)], axis=1)
        return jnp.dot(wide, weights[...], preferred_element_type=jnp.float32)

    loads[0].wait()
    loads[1].wait()
    for row, side in ((0, 1), (rows - 1, 0)):
        x = silu(state[row])
        halo_send_one[side] = x.astype(jnp.bfloat16)
        store_taps(taps_one, row + 1, x)
    loads[2].wait()

    def silu_row(row, _):
        store_taps(taps_one, row + 1, silu(state[row]))
        return 0

    lax.fori_loop(1, rows - 1, silu_row, 0)

    for load in loads[3:9]:
        load.wait()

    def finish_one(row, added):
        x = state[row] + added
        state[row] = x
        store_taps(taps_two, row + 1, silu(x))

    def conv_one_step(step, _):
        first = 1 + 2 * step
        added = conv_pair(taps_one, kernel_one, first)
        for o in range(2):
            finish_one(first + o, added[:, o * channels : (o + 1) * channels])
        return 0

    lax.fori_loop(0, rows // 2 - 1, conv_one_step, 0)

    def one_copy(g, k):
        first = PAIR_STARTS[g]
        return pltpu.make_async_remote_copy(
            src_ref=normed.at[pl.ds(first, 2), pl.ds(pl.multiple_of(other(k) * chunk, chunk), chunk)],
            dst_ref=gathers[g].at[view],
            send_sem=one_ssem.at[g, k],
            recv_sem=one_rsem.at[g, view],
            device_id={"view": other(k)},
            device_id_type=MESH,
        )

    def one_arrival(g, k):
        return pltpu.make_async_remote_copy(
            src_ref=gathers[g].at[other(k)],
            dst_ref=gathers[g].at[other(k)],
            send_sem=one_ssem.at[g, k],
            recv_sem=one_rsem.at[g, other(k)],
            device_id={"view": other(k)},
            device_id_type=MESH,
        )

    def conv_two_pair(first):
        added = conv_pair(taps_two, kernel_two, first)
        for o in range(2):
            x = state[first + o] + added[:, o * channels : (o + 1) * channels]
            state[first + o] = x
            scale = lax.rsqrt(jnp.mean(x * x, axis=-1, keepdims=True) + epsilon)
            normed[first + o] = (x * scale * gains[0]).astype(jnp.bfloat16)

    def scatter(g):
        for k in range(1, views):
            one_copy(g, k).start()

    loads[22].wait()
    for load in loads[9:15]:
        load.wait()

    def conv_two_inner(step, _):
        conv_two_pair(2 + 2 * step)
        for g in range(2):

            @pl.when(step == g)
            def _():
                if g == 0:
                    pl.semaphore_wait(barrier, views + 1)
                    for side in range(2):
                        pl.when(leaves[side])(halo_copy(0, side, halo_send_one, halo_recv_one).start)
                scatter(g)

        return 0

    lax.fori_loop(0, 2, conv_two_inner, 0)

    for load in loads[15:22] + loads[23:]:
        load.wait()
    factor = 1.0 / math.sqrt(channels) * math.log2(math.e)
    for c in range(columns // 128):
        at = slice(c * 128, (c + 1) * 128)
        turned = jnp.concatenate([temper_in[:, at] * factor] * (128 // rows), axis=0).T
        for row in range(rows):
            temper_wide[row, at, :] = jnp.broadcast_to(turned[:, row : row + 1], (128, channels))

    def fill_ones(row, _):
        for p in range(2):
            at = pl.ds(pl.multiple_of(row * columns, columns), columns)
            values[p, at, channels : 2 * channels] = jnp.ones((columns, channels), jnp.bfloat16)
        return 0

    lax.fori_loop(0, rows + 2, fill_ones, 0)

    own = pl.ds(pl.multiple_of(view * chunk, chunk), chunk)

    def two_copy(row, k):
        return pltpu.make_async_remote_copy(
            src_ref=deal.at[row, k],
            dst_ref=pair.at[:, row + 1, own],
            send_sem=two_ssem.at[row, k],
            recv_sem=two_rsem.at[row, view],
            device_id={"view": other(k)},
            device_id_type=MESH,
        )

    def two_arrival(row, k):
        theirs = pl.ds(pl.multiple_of(other(k) * chunk, chunk), chunk)
        return pltpu.make_async_remote_copy(
            src_ref=deal.at[row, k],
            dst_ref=pair.at[:, row + 1, theirs],
            send_sem=two_ssem.at[row, k],
            recv_sem=two_rsem.at[row, other(k)],
            device_id={"view": other(k)},
            device_id_type=MESH,
        )

    def gathered(g):
        gathers[g][view] = normed[pl.ds(PAIR_STARTS[g], 2), own]
        for k in range(1, views):
            one_arrival(g, k).wait_recv()

    def deal_row(row):
        g = PAIR_STARTS.index(row - row % 2)
        for k in range(1, views):
            for p in range(2):
                deal[row, k, p] = gathers[g][partners_in[p, other(k)], row % 2]
        for p in range(2):
            pair[p, row + 1, own] = gathers[g][partners_in[p, view], row % 2]
        for k in range(1, views):
            two_copy(row, k).start()

    gathered(0)
    deal_row(3)
    for side in range(2):
        pl.when(enters[side])(halo_copy(0, side, halo_send_one, halo_recv_one).wait_recv)
    edge_taps(taps_one, halo_recv_one)

    def conv_one_edge(step, _):
        row = (rows - 1) * step
        wide = jnp.concatenate([taps_one[row + i] for i in range(3)], axis=1)
        finish_one(
            row,
            jnp.dot(
                wide,
                kernel_one[0 : 9 * channels, 0:channels],
                preferred_element_type=jnp.float32,
            ),
        )
        return 0

    lax.fori_loop(0, 2, conv_one_edge, 0)
    halo_send_two[0] = taps_two[rows, :, channels : 2 * channels]
    halo_send_two[1] = taps_two[1, :, channels : 2 * channels]
    for side in range(2):
        pl.when(leaves[side])(halo_copy(1, side, halo_send_two, halo_recv_two).start)

    gathered(1)
    deal_row(4)
    deal_row(2)
    deal_row(5)

    def query_row(row, _):
        query[row] = jnp.dot(
            normed[row], query_w[...], preferred_element_type=jnp.float32
        ).astype(jnp.bfloat16)
        return 0

    lax.fori_loop(2, rows - 2, query_row, 0)

    for side in range(2):
        pl.when(enters[side])(halo_copy(1, side, halo_send_two, halo_recv_two).wait_recv)
    edge_taps(taps_two, halo_recv_two)

    def conv_two_edge(step, _):
        conv_two_pair((rows - 2) * step)
        for g in range(2):

            @pl.when(step == g)
            def _():
                scatter(g + 2)

        return 0

    lax.fori_loop(0, 2, conv_two_edge, 0)

    lax.fori_loop(0, 2, query_row, 0)
    lax.fori_loop(rows - 2, rows, query_row, 0)

    def edge_copy(side, k):
        source, target = ((rows, 0), (1, rows + 1))[side]
        at = pl.ds(pl.multiple_of(other(k) * chunk, chunk), chunk)
        return pltpu.make_async_remote_copy(
            src_ref=pair.at[:, source, at],
            dst_ref=pair.at[:, target, at],
            send_sem=edge_ssem.at[side, k],
            recv_sem=edge_rsem.at[side, k],
            device_id={"band": down if side == 0 else up},
            device_id_type=MESH,
        )

    def pick(table, step):
        packed = sum(entry << (4 * n) for n, entry in enumerate(table[:7]))
        rest = sum(entry << (4 * n) for n, entry in enumerate(table[7:]))
        late = step // 7
        word = (1 - late) * packed + late * rest
        return lax.shift_right_logical(word, 4 * (step - 7 * late)) % 16

    def store_out(row):
        return pltpu.make_async_copy(out_stage.at[row], out_ref.at[0, row], store_sem.at[row])

    def attend(step, _):
        row = pick(ATTENDED, step)
        place_in = pick([r + 1 for r in ARRIVALS], step)
        for n, r in enumerate(ARRIVALS):

            @pl.when(step == n)
            def _(n=n, r=r):
                if n == 3:
                    gathered(2)
                    deal_row(1)
                    deal_row(0)
                if n == 4:
                    gathered(3)
                    deal_row(6)
                    deal_row(7)
                if 0 <= r < rows:
                    side = {0: 1, rows - 1: 0}.get(r)
                    if side is not None:
                        pl.when(leaves[side])(edge_copy(side, 0).start)
                    for k in range(1, views):
                        two_arrival(r, k).wait_recv()
                        if side is not None:
                            pl.when(leaves[side])(edge_copy(side, k).start)
                else:
                    side = 1 if r == rows else 0

                    @pl.when(enters[side])
                    def _():
                        for k in range(views):
                            edge_copy(side, k).wait_recv()

                    @pl.when(jnp.logical_not(enters[side]))
                    def _():
                        pair[:, r + 1] = jnp.zeros((2, columns, channels), jnp.bfloat16)

        for p in range(2):
            both = jnp.dot(pair[p, place_in], kv_w[...], preferred_element_type=jnp.float32)
            both = both.astype(jnp.bfloat16)
            at = pl.ds(pl.multiple_of(place_in * columns, columns), columns)
            keys[p, at] = both[:, 0:channels]
            values[p, at, 0:channels] = both[:, channels : 2 * channels]

        @pl.when(step >= 2)
        def _():
            attend_row(row)
            store_out(row).start()

        return 0

    def attend_row(row):
        blended = []
        window = pl.ds(pl.multiple_of(row * columns, columns), 3 * columns)
        for p in range(2):
            scores[p] = lax.dot_general(
                query[row],
                keys[p, window],
                (((1,), (1,)), ((), ())),
                preferred_element_type=jnp.float32,
            )
        for p in range(2):
            for k in range(columns // strip):
                at = slice(k * strip, (k + 1) * strip)
                temper = temper_wide[row, at]
                lanes = range(3 * columns // 128)
                parts = [scores[p, at, j * 128 : (j + 1) * 128] for j in lanes]
                peak = functools.reduce(jnp.maximum, parts)
                top = jnp.max(peak, axis=-1, keepdims=True) * temper
                for j in lanes:
                    lifted = jnp.exp2(parts[j] * temper - top)
                    shares[p, at, j * 128 : (j + 1) * 128] = lifted.astype(jnp.bfloat16)
            total = jnp.dot(shares[p], values[p, window], preferred_element_type=jnp.float32)
            blended.append((total[:, 0:channels] / total[:, channels:]).astype(jnp.bfloat16))
        message = jnp.dot(
            jnp.concatenate(blended, axis=1), out_w2[...], preferred_element_type=jnp.float32
        )
        scale = lax.rsqrt(jnp.mean(message * message, axis=-1, keepdims=True) + epsilon)
        out_stage[row] = state[row] + message * scale * gains[1]

    lax.fori_loop(0, rows + 2, attend, 0)

    for side in range(2):
        pl.when(leaves[side])(halo_copy(0, side, halo_send_one, halo_recv_one).wait_send)
        pl.when(leaves[side])(halo_copy(1, side, halo_send_two, halo_recv_two).wait_send)
        for k in range(views):
            pl.when(leaves[side])(edge_copy(side, k).wait_send)
    for g in range(4):
        for k in range(1, views):
            one_copy(g, k).wait_send()
    for row in range(rows):
        store_out(row).wait()
        for k in range(1, views):
            two_copy(row, k).wait_send()


def hand_over(source, target, stage, in_sem, out_sem):
    count = stage.shape[0]
    reads = [
        pltpu.make_async_copy(source.at[0, i], stage.at[i], in_sem.at[i]) for i in range(count)
    ]
    writes = [
        pltpu.make_async_copy(stage.at[i], target.at[0, i], out_sem.at[i]) for i in range(count)
    ]
    for read in reads:
        read.start()
    for read, write in zip(reads, writes):
        read.wait()
        write.start()
    for write in writes:
        write.wait()


def per_device(views, bands, features, tempers, partners, *weights):
    conv_one, conv_two, query_w, key_w, value_w, out_w, norm_gain, message_gain = weights
    _, rows, columns, channels = features.shape
    chunk = columns // views
    half = jnp.bfloat16
    full = jnp.float32
    any_space = pl.BlockSpec(memory_space=pl.ANY)
    dma = pltpu.SemaphoreType.DMA
    line = (columns, channels)
    refined = pl.pallas_call(
        functools.partial(kernel, views, bands),
        out_shape=jax.ShapeDtypeStruct(features.shape, full),
        in_specs=[any_space] * 11,
        out_specs=any_space,
        scratch_shapes=[
            pltpu.VMEM((rows, columns), full),
            pltpu.SMEM((2, views), jnp.int32),
            pltpu.VMEM((2, 1, channels), full),
            pltpu.VMEM((rows,) + line, full),
            pltpu.VMEM((rows,) + line, full),
            pltpu.VMEM((rows + 2, columns, 3 * channels), half),
            pltpu.VMEM((rows + 2, columns, 3 * channels), half),
            pltpu.VMEM((12 * channels, 2 * channels), half),
            pltpu.VMEM((12 * channels, 2 * channels), half),
            pltpu.VMEM((channels, channels), half),
            pltpu.VMEM((channels, 2 * channels), half),
            pltpu.VMEM((2 * channels, channels), half),
            pltpu.VMEM((2,) + line, half),
            pltpu.VMEM((2,) + line, half),
            pltpu.VMEM((2,) + line, half),
            pltpu.VMEM((2,) + line, half),
            pltpu.VMEM((rows,) + line, half),
            pltpu.VMEM((views, 2, chunk, channels), half),
            pltpu.VMEM((views, 2, chunk, channels), half),
            pltpu.VMEM((views, 2, chunk, channels), half),
            pltpu.VMEM((views, 2, chunk, channels), half),
            pltpu.VMEM((rows, views, 2, chunk, channels), half),
            pltpu.VMEM((2, rows + 2) + line, half),
            pltpu.VMEM((rows,) + line, half),
            pltpu.VMEM((2, (rows + 2) * columns, channels), half),
            pltpu.VMEM((2, (rows + 2) * columns, 2 * channels), half),
            pltpu.VMEM((rows,) + line, full),
            pltpu.VMEM((2, columns, 3 * columns), full),
            pltpu.VMEM((2, columns, 3 * columns), half),
            dma((24,)),
            dma((rows,)),
            dma((2, 2)),
            dma((2, 2)),
            dma((4, views)),
            dma((4, views)),
            dma((rows, views)),
            dma((rows, views)),
            dma((2, views)),
            dma((2, views)),
        ],
        compiler_params=pltpu.CompilerParams(
            collective_id=0, has_side_effects=True, vmem_limit_bytes=60 * 1024 * 1024
        ),
    )(
        features,
        tempers,
        partners.T,
        conv_one.reshape(3, 3 * channels, channels),
        conv_two.reshape(3, 3 * channels, channels),
        query_w,
        key_w,
        value_w,
        out_w,
        norm_gain.reshape(1, channels),
        message_gain.reshape(1, channels),
    )
    return pl.pallas_call(
        hand_over,
        out_shape=jax.ShapeDtypeStruct(features.shape, full),
        in_specs=[any_space],
        out_specs=any_space,
        scratch_shapes=[pltpu.VMEM((rows,) + line, full), dma((rows,)), dma((rows,))],
        compiler_params=pltpu.CompilerParams(vmem_limit_bytes=60 * 1024 * 1024),
    )(refined)


def solution(mesh):
    whole = P()
    in_specs = (
        P("view", "band", None, None),
        P("view", "band", None),
    ) + (whole,) * 9
    return jax.shard_map(
        functools.partial(per_device, mesh.shape["view"], mesh.shape["band"]),
        mesh=mesh,
        in_specs=in_specs,
        out_specs=P("view", "band", None, None),
        check_vma=False,
    )
```
